512 devices in a mesh: dp: 16 (over z, x_lo), space: 32 (over x_hi, y, core).
Axes of the slice: x: 4 (x_hi: 2, x_lo: 2; x = x_hi * 2 + x_lo), y: 8, z: 8, core: 2. Of those that a mesh axis runs over, the one named last changes fastest.
Arguments:
- pre_act: bfloat16 [16, 256, 128, 320], P('dp', 'space'), may hold values from -6 to 6
- out_grad: bfloat16 [16, 256, 128, 320], P('dp', 'space'), may hold values from -6 to 6
- kernel: bfloat16 [3, 3, 320, 320], replicated, may hold values from -0.109375 to 0.109375
Outputs:
- in_grad: bfloat16 [16, 256, 128, 320], P('dp', 'space')
- kernel_grad: float32 [2880, 320], P('dp')
The draws below stay inside these ranges and needn't reach their ends.
All inputs are finite; a program needn't handle non-finite values.
Results may differ from the reference program's by a relative error of at most 0.0029.
Values may be sent and summed in bfloat16 or wider, within the bound.
A program may use at most 64 MiB of HBM per device.

```python
import jax
import jax.numpy as jnp
from jax import lax

C = 320
COLS = 128
IMAGES = 16
HEIGHT = 256


def strengthened(drawn, own_key, source, target, shards_of, factor):
    def block_of(axis_at):
        return (jnp.arange(drawn.shape[axis_at]) // (drawn.shape[axis_at] // shards_of)).reshape((-1,) + (1,) * (drawn.ndim - 1 - axis_at))

    one_side = jax.random.permutation(own_key, shards_of)[block_of(target)]
    far = (block_of(target) + shards_of // 2) % shards_of
    return jnp.where((block_of(source) == one_side) | (block_of(source) == far), factor * drawn, drawn)


def level_of(own_key, dims, split, low, top_value):
    level, own = 1.0, jax.random.fold_in(own_key, 6)
    for position, parts in split:
        draws = jnp.exp(jax.random.uniform(jax.random.fold_in(own, position), (parts,), jnp.float32, low / len(split), top_value / len(split)))
        level = level * jnp.repeat(draws, dims[position] // parts).reshape([-1 if axis == position else 1 for axis in range(len(dims))])
    return level


def normal_values(rng, extent, scale, most, shards=(), held_as=jnp.bfloat16):
    values = scale * jax.random.normal(rng, extent, jnp.float32)
    if shards:
        values = values * level_of(rng, extent, shards, -0.22, 0.18)
    return jnp.clip(values, -most, most).astype(held_as)


def gaussian_with(stream_key, extent, scale, reach, cuts, heavy, dtype=jnp.bfloat16):
    values = scale * jax.random.normal(stream_key, extent, jnp.float32)
    if cuts:
        values = values * level_of(stream_key, extent, cuts, -0.22, 0.18)
    return jnp.clip(strengthened(values, jax.random.fold_in(stream_key, 3), *heavy), -reach, reach).astype(dtype)


def setup_inputs(seed: int = 0) -> dict:
    keys = jax.random.split(jax.random.key(seed), 4)
    return {
        "pre_act": gaussian_with(keys[0], (IMAGES, HEIGHT, COLS, C), 1.0, 6.0, ((0, 16), (1, 32)), (0, 3, 16, 2.0)),
        "out_grad": normal_values(keys[1], (IMAGES, HEIGHT, COLS, C), 1.0, 6.0, ((0, 16), (1, 32))),
        "kernel": normal_values(keys[2], (3, 3, C, C), (9 * C) ** -0.5, 0.109375),
    }


def reference(pre_act, out_grad, kernel):
    height = pre_act.shape[1]
    width = pre_act.shape[2]
    chans = pre_act.shape[3]

    def one_image(carry, pair):
        feats, grads = pair
        xf = feats.astype(jnp.float32)
        act = jax.nn.silu(xf).astype(jnp.bfloat16)
        act_pad = jnp.pad(act, ((1, 1), (1, 1), (0, 0)))
        grad_pad = jnp.pad(grads, ((1, 1), (1, 1), (0, 0)))
        g_flat = grads.reshape(height * width, chans)
        act_grad = jnp.zeros((height * width, chans), jnp.float32)
        new_carry = carry
        for tap_a in range(3):
            for tap_b in range(3):
                shifted = grad_pad[2 - tap_a:2 - tap_a + height, 2 - tap_b:2 - tap_b + width, :].reshape(height * width, chans)
                act_grad = act_grad + jnp.dot(shifted, kernel[tap_a, tap_b].T, preferred_element_type=jnp.float32)
                window = act_pad[tap_a:tap_a + height, tap_b:tap_b + width, :].reshape(height * width, chans)
                term = jnp.dot(window.T, g_flat, preferred_element_type=jnp.float32)
                new_carry = new_carry.at[tap_a, tap_b].add(term)
        sig = jax.nn.sigmoid(xf)
        deriv = sig * (1.0 + xf * (1.0 - sig))
        in_grad = (act_grad.reshape(height, width, chans) * deriv).astype(jnp.bfloat16)
        return new_carry, in_grad

    start = jnp.zeros((3, 3, chans, chans), jnp.float32)
    total, in_grad = lax.scan(one_image, start, (pre_act, out_grad))
    pixels = pre_act.shape[0] * height * width
    scaled = total * (float(pixels) ** -0.5)
    kernel_grad = jnp.transpose(scaled, (2, 0, 1, 3)).reshape(9 * chans, chans)
    return in_grad, kernel_grad
```

```python
import functools

import jax
import jax.numpy as jnp
from jax import lax
from jax.experimental import pallas as pl
from jax.experimental.pallas import tpu as pltpu
from jax.sharding import PartitionSpec as P

MESH = pl.DeviceIdType.MESH
F32 = jnp.float32
BF16 = jnp.bfloat16

NX, NY, NZ = 4, 8, 8
ROWS, C, W = 8, 320, 128
BLK = 20
PARTS = ((1, "z"), (0, "x"), (2, "x"))


def nearest_last(n):
    steps = []
    for k in range(n // 2, 0, -1):
        steps.append(k)
        if n - k != k:
            steps.append(n - k)
    return steps


def kernel(
    scale, pre_hbm, og_hbm, k_hbm, in_hbm, kg_hbm,
    pre_v, og_v, k_v, in_v, act2, og2, tap_sum, part_sum,
    snd0, rcv0, snd_x, rcv_x, snd_z, rcv_z,
    sndx2, rcvx2, sndz2, rcvz2, ybuf, fin,
    load_sem, store_sem, halo_s, halo_r, c_s, c_r, x_s, x_r, z_s, z_r,
    x2_s, x2_r, z2_s, z2_r, y_s, y_r, f_s, f_r,
):
    dp = lax.axis_index("dp")
    sp = lax.axis_index("space")
    z = dp // 2
    xlo = lax.rem(dp, 2)
    core = lax.rem(sp, 2)
    y = lax.rem(sp // 2, NY)
    xhi = sp // (2 * NY)
    x = xhi * 2 + xlo

    def dev(z_, x_, y_, core_):
        return {"dp": z_ * 2 + lax.rem(x_, 2), "space": ((x_ // 2) * NY + y_) * 2 + core_}

    def xp(k):
        return lax.rem(x + k, NX)

    def yp(k):
        return lax.rem(y + k, NY)

    def zp(k):
        return lax.rem(z + k, NZ)

    up = {"dp": dp, "space": lax.rem(sp + 31, 32)}
    down = {"dp": dp, "space": lax.rem(sp + 1, 32)}
    mate = dev(z, x, y, 1 - core)
    far = dev(z, xp(2), y, core)
    far_mate = dev(z, xp(2), y, 1 - core)

    loads = [
        pltpu.make_async_copy(og_hbm, og_v.at[pl.ds(1, ROWS)], load_sem.at[0]),
        pltpu.make_async_copy(pre_hbm, pre_v, load_sem.at[1]),
        pltpu.make_async_copy(k_hbm, k_v, load_sem.at[2]),
    ]
    for c in loads:
        c.start()

    barrier = pltpu.get_barrier_semaphore()
    greeted = [up, down, far_mate]
    greeted += [dev(z, xp(k), y, core) for k in range(1, NX)]
    greeted += [dev(z, x, yp(k), core) for k in range(1, NY)]
    greeted += [dev(zp(k), x, y, core) for k in range(1, NZ)]
    for d in greeted:
        pl.semaphore_signal(barrier, inc=1, device_id=d, device_id_type=MESH)

    def shifts(r, value):
        lanes = pl.ds(r * W, W)
        og2[1, :, lanes] = value
        wide = value.astype(F32)
        col = lax.broadcasted_iota(jnp.int32, (C, W), 1)
        og2[0, :, lanes] = jnp.where(col == W - 1, 0.0, pltpu.roll(wide, W - 1, 1)).astype(BF16)
        og2[2, :, lanes] = jnp.where(col == 0, 0.0, pltpu.roll(wide, 1, 1)).astype(BF16)

    loads[0].wait()
    for r in range(1, ROWS + 1):
        shifts(r, og_v[r])
    loads[1].wait()
    for r in range(ROWS):
        v = pre_v[r].astype(F32)
        act2[:, pl.ds(r * W, W)] = (v * (1.0 / (1.0 + jnp.exp(-v)))).astype(BF16)

    pl.semaphore_wait(barrier, len(greeted))

    halos = [
        pltpu.make_async_remote_copy(
            src_ref=og_hbm.at[ROWS - 1], dst_ref=og_v.at[0], send_sem=halo_s.at[0], recv_sem=halo_r.at[0],
            device_id=down, device_id_type=MESH),
        pltpu.make_async_remote_copy(
            src_ref=og_hbm.at[0], dst_ref=og_v.at[ROWS + 1], send_sem=halo_s.at[1], recv_sem=halo_r.at[1],
            device_id=up, device_id_type=MESH),
    ]
    for c in halos:
        c.start()

    def tap_row(p, a):
        for b in range(3):
            tap_sum[b] = lax.dot_general(
                act2[...], og2[b, :, pl.ds((2 - a) * W, ROWS * W)],
                (((1,), (1,)), ((), ())), preferred_element_type=F32)
        for blk in range(16):
            for b in range(3):
                part_sum[p, blk // 2, blk % 2, pl.ds(b * BLK, BLK), :] = tap_sum[b, pl.ds(blk * BLK, BLK), :]
            part_sum[p, blk // 2, blk % 2, pl.ds(3 * BLK, 4), :] = jnp.zeros((4, C), F32)

    def core_copy(p):
        return pltpu.make_async_remote_copy(
            src_ref=snd0.at[p], dst_ref=rcv0.at[p], send_sem=c_s.at[p], recv_sem=c_r.at[p],
            device_id=mate, device_id_type=MESH)

    def core_send(p):
        for zb in range(NZ):
            for xl in range(2):
                for half in range(2):
                    rows = pl.ds(pl.multiple_of((1 - core) * 32 + half * 16, 16), 16)
                    snd0[p, zb, xl, half] = part_sum[p, zb, xl, rows, :].astype(BF16)
        core_copy(p).start()

    def chip_rows(p, zb, xl, half):
        mine = part_sum[p, zb, xl, pl.ds(pl.multiple_of(core * 32 + half * 16, 16), 16), :]
        return mine + rcv0[p, zb, xl, half].astype(F32)

    def first_copy(p, i, k):
        if PARTS[p][1] == "x":
            q = p - 1
            peer = xp(k)
            return pltpu.make_async_remote_copy(
                src_ref=snd_x.at[q, peer], dst_ref=rcv_x.at[q, x], send_sem=x_s.at[q, i], recv_sem=x_r.at[q, x],
                device_id=dev(z, peer, y, core), device_id_type=MESH), peer
        peer = zp(k)
        return pltpu.make_async_remote_copy(
            src_ref=snd_z.at[peer], dst_ref=rcv_z.at[z], send_sem=z_s.at[i], recv_sem=z_r.at[z],
            device_id=dev(peer, x, y, core), device_id_type=MESH), peer

    def first_recv(p, peer):
        if PARTS[p][1] == "x":
            q = p - 1
            return pltpu.make_async_remote_copy(
                src_ref=snd_x.at[q, peer], dst_ref=rcv_x.at[q, peer], send_sem=x_s.at[q, 0], recv_sem=x_r.at[q, peer],
                device_id=mate, device_id_type=MESH)
        return pltpu.make_async_remote_copy(
            src_ref=snd_z.at[peer], dst_ref=rcv_z.at[peer], send_sem=z_s.at[0], recv_sem=z_r.at[peer],
            device_id=mate, device_id_type=MESH)

    def first_steps(p):
        return nearest_last(NX if PARTS[p][1] == "x" else NZ)

    def first_send(p):
        core_copy(p).wait_recv()
        if PARTS[p][1] == "x":
            for zb in range(NZ):
                for xx in range(NX):
                    snd_x[p - 1, xx, zb] = chip_rows(p, zb, xx % 2, xx // 2).astype(BF16)
        else:
            for zb in range(NZ):
                for xx in range(NX):
                    snd_z[zb, xx] = chip_rows(p, zb, xx % 2, xx // 2).astype(BF16)
        for i, k in enumerate(first_steps(p)):
            first_copy(p, i, k)[0].start()

    def second_copy(p, i, k):
        if PARTS[p][1] == "x":
            q = p - 1
            peer = zp(k)
            return pltpu.make_async_remote_copy(
                src_ref=sndz2.at[q, peer], dst_ref=rcvz2.at[q, z], send_sem=z2_s.at[q, i], recv_sem=z2_r.at[q, z],
                device_id=dev(peer, x, y, core), device_id_type=MESH), peer
        peer = xp(k)
        return pltpu.make_async_remote_copy(
            src_ref=sndx2.at[peer], dst_ref=rcvx2.at[x], send_sem=x2_s.at[i], recv_sem=x2_r.at[x],
            device_id=dev(z, peer, y, core), device_id_type=MESH), peer

    def second_recv(p, peer):
        if PARTS[p][1] == "x":
            q = p - 1
            return pltpu.make_async_remote_copy(
                src_ref=sndz2.at[q, peer], dst_ref=rcvz2.at[q, peer], send_sem=z2_s.at[q, 0], recv_sem=z2_r.at[q, peer],
                device_id=mate, device_id_type=MESH)
        return pltpu.make_async_remote_copy(
            src_ref=sndx2.at[peer], dst_ref=rcvx2.at[peer], send_sem=x2_s.at[0], recv_sem=x2_r.at[peer],
            device_id=mate, device_id_type=MESH)

    def second_steps(p):
        return nearest_last(NZ if PARTS[p][1] == "x" else NX)

    def second_send(p):
        for k in first_steps(p):
            peer = xp(k) if PARTS[p][1] == "x" else zp(k)
            first_recv(p, peer).wait_recv()
        if PARTS[p][1] == "x":
            q = p - 1
            for zb in range(NZ):
                total = chip_rows(p, zb, xlo, xhi)
                for k in range(1, NX):
                    total = total + rcv_x[q, xp(k), zb].astype(F32)
                sndz2[q, zb] = total
        else:
            for xx in range(NX):
                total = chip_rows(p, z, xx % 2, xx // 2)
                for k in range(1, NZ):
                    total = total + rcv_z[zp(k), xx].astype(F32)
                sndx2[xx] = total
        for i, k in enumerate(second_steps(p)):
            second_copy(p, i, k)[0].start()

    def y_copy(p, i, k):
        peer = yp(k)
        return pltpu.make_async_remote_copy(
            src_ref=ybuf.at[p, y], dst_ref=ybuf.at[p, y], send_sem=y_s.at[p, i], recv_sem=y_r.at[p, y],
            device_id=dev(z, x, peer, core), device_id_type=MESH)

    def y_recv(p, peer):
        return pltpu.make_async_remote_copy(
            src_ref=ybuf.at[p, peer], dst_ref=ybuf.at[p, peer], send_sem=y_s.at[p, 0], recv_sem=y_r.at[p, peer],
            device_id=mate, device_id_type=MESH)

    def y_send(p):
        for k in second_steps(p):
            peer = zp(k) if PARTS[p][1] == "x" else xp(k)
            second_recv(p, peer).wait_recv()
        if PARTS[p][1] == "x":
            q = p - 1
            total = sndz2[q, z]
            for k in range(1, NZ):
                total = total + rcvz2[q, zp(k)]
        else:
            total = sndx2[x]
            for k in range(1, NX):
                total = total + rcvx2[xp(k)]
        ybuf[p, y] = (total * scale).astype(BF16)
        for i, k in enumerate(nearest_last(NY)):
            y_copy(p, i, k).start()

    def f_copies(p):
        slot = fin.at[p, core, xhi]
        return [
            pltpu.make_async_remote_copy(
                src_ref=slot, dst_ref=slot, send_sem=f_s.at[p, i], recv_sem=f_r.at[p, i],
                device_id=d, device_id_type=MESH)
            for i, d in enumerate((far_mate, far, mate))
        ]

    def f_recvs(p):
        slots = ((1 - core, 1 - xhi), (core, 1 - xhi), (1 - core, xhi))
        return [
            pltpu.make_async_remote_copy(
                src_ref=fin.at[p, cc, hh], dst_ref=fin.at[p, cc, hh], send_sem=f_s.at[p, i], recv_sem=f_r.at[p, i],
                device_id=mate, device_id_type=MESH)
            for i, (cc, hh) in enumerate(slots)
        ]

    def f_send(p):
        for k in nearest_last(NY):
            y_recv(p, yp(k)).wait_recv()
        total = ybuf[p, 0].astype(F32)
        for yy in range(1, NY):
            total = total + ybuf[p, yy].astype(F32)
        fin[p, core, xhi] = total
        for c in f_copies(p):
            c.start()

    def in_grad(pair):
        lanes = pair * 2 * W
        total = jnp.zeros((C, 2 * W), F32)
        for a in range(3):
            for b in range(3):
                total = total + jnp.dot(
                    k_v[a, b], og2[b, :, pl.ds((2 - a) * W + lanes, 2 * W)], preferred_element_type=F32)
        for i in range(2):
            v = pre_v[pair * 2 + i].astype(F32)
            s = 1.0 / (1.0 + jnp.exp(-v))
            in_v[pair * 2 + i] = (total[:, i * W : (i + 1) * W] * (s * (1.0 + v * (1.0 - s)))).astype(BF16)

    tap_row(0, PARTS[0][0])
    core_send(0)
    for i, (c, edge) in enumerate(zip(halos, (sp == 0, sp == 31))):
        c.wait_recv()
        r = i * (ROWS + 1)
        shifts(r, jnp.where(edge, jnp.zeros((C, W), BF16), og_v[r]))
    first_send(0)
    tap_row(1, PARTS[1][0])
    core_send(1)
    tap_row(2, PARTS[2][0])
    first_send(1)
    core_send(2)
    loads[2].wait()
    in_grad(0)
    first_send(2)
    in_grad(1)
    in_grad(2)
    second_send(1)
    in_grad(3)
    in_store = pltpu.make_async_copy(in_v, in_hbm, store_sem.at[0])
    in_store.start()
    second_send(0)
    second_send(2)
    y_send(0)
    y_send(1)
    y_send(2)
    for p in range(3):
        f_send(p)
    stores = []
    for p in range(3):
        for c in f_recvs(p):
            c.wait_recv()
        c = pltpu.make_async_copy(fin.at[p], kg_hbm.at[PARTS[p][0]], store_sem.at[1 + p])
        c.start()
        stores.append(c)

    for c in halos:
        c.wait_send()
    for p in range(3):
        core_copy(p).wait_send()
        for i, k in enumerate(first_steps(p)):
            first_copy(p, i, k)[0].wait_send()
        for i, k in enumerate(second_steps(p)):
            second_copy(p, i, k)[0].wait_send()
        for i, k in enumerate(nearest_last(NY)):
            y_copy(p, i, k).wait_send()
        for c in f_copies(p):
            c.wait_send()
    in_store.wait()
    for c in stores:
        c.wait()


def shards(scale, pre_act, out_grad, weights):
    to_rows = lambda t: jnp.swapaxes(t[0], 1, 2)
    vm, sem = pltpu.VMEM, pltpu.SemaphoreType.DMA
    grad, sums = pl.pallas_call(
        functools.partial(kernel, scale),
        out_shape=(
            jax.ShapeDtypeStruct((ROWS, C, W), BF16),
            jax.ShapeDtypeStruct((3, 2, 2, 16, C), F32),
        ),
        in_specs=[pl.BlockSpec(memory_space=pl.ANY)] * 3,
        out_specs=(pl.BlockSpec(memory_space=pl.ANY),) * 2,
        scratch_shapes=[
            vm((ROWS, C, W), BF16),
            vm((ROWS + 2, C, W), BF16),
            vm((3, 3, C, C), BF16),
            vm((ROWS, C, W), BF16),
            vm((C, ROWS * W), BF16),
            vm((3, C, (ROWS + 2) * W), BF16),
            vm((3, C, C), F32),
            vm((3, NZ, 2, 64, C), F32),
            vm((3, NZ, 2, 2, 16, C), BF16),
            vm((3, NZ, 2, 2, 16, C), BF16),
            vm((2, NX, NZ, 16, C), BF16),
            vm((2, NX, NZ, 16, C), BF16),
            vm((NZ, NX, 16, C), BF16),
            vm((NZ, NX, 16, C), BF16),
            vm((NX, 16, C), F32),
            vm((NX, 16, C), F32),
            vm((2, NZ, 16, C), F32),
            vm((2, NZ, 16, C), F32),
            vm((3, NY, 16, C), BF16),
            vm((3, 2, 2, 16, C), F32),
            sem((3,)), sem((4,)), sem((2,)), sem((2,)), sem((3,)), sem((3,)),
            sem((2, 3)), sem((2, NX)), sem((7,)), sem((NZ,)),
            sem((3,)), sem((NX,)), sem((2, 7)), sem((2, NZ)),
            sem((3, 7)), sem((3, NY)), sem((3, 3)), sem((3, 3)),
        ],
        compiler_params=pltpu.CompilerParams(collective_id=0, has_side_effects=True),
    )(to_rows(pre_act), to_rows(out_grad), weights)
    in_grad = jnp.swapaxes(grad, 1, 2)[None]
    sums = sums.reshape(3, 64, C)[:, : 3 * BLK].reshape(9, BLK, C)
    return in_grad, jnp.swapaxes(sums, 0, 1).reshape(9 * BLK, C)


def solution(mesh):
    placed = P("dp", "space", None, None)

    def whole(pre_act, out_grad, weights):
        pixels = pre_act.shape[0] * pre_act.shape[1] * pre_act.shape[2]
        return jax.shard_map(
            functools.partial(shards, float(pixels) ** -0.5),
            mesh=mesh,
            in_specs=(placed, placed, P()),
            out_specs=(placed, P("dp", None)),
            check_vma=False,
        )(pre_act, out_grad, weights)

    return whole
```

```python
import functools

import jax
import jax.numpy as jnp
from jax import lax
from jax.experimental import pallas as pl
from jax.experimental.pallas import tpu as pltpu
from jax.sharding import PartitionSpec as P

MESH = pl.DeviceIdType.MESH
F32 = jnp.float32
BF16 = jnp.bfloat16

NX, NY, NZ = 4, 8, 8
ROWS, C, W = 8, 320, 128
BLK = 20
ZROWS = 2 * BLK
LANES, TILES = 1024, 8
BF16, SECOND_T, BF16 = BF16, F32, BF16
PARTS = (1, 0, 2)
ZROWS = 2 * BLK
XROWS = (16, 32, 24)
LANES, TILES = 1024, 8


def nearest_last(n):
    steps = []
    for k in range(n // 2, 0, -1):
        steps.append(k)
        if n - k != k:
            steps.append(n - k)
    return steps


def kernel(
    scale, pre_hbm, og_hbm, k_hbm, in_hbm, kg_hbm,
    pre_v, og_v, k_v, in_v, kg_v, act2, og2, part_sum,
    rcv0, snd_x, rcv_x, snd_z, rcv_z,
    sndx2, rcvx2, sndz2, rcvz2, own2, ybuf, done, fin,
    load_sem, store_sem, halo_s, halo_r, c_s, c_r, x_s, x_r, z_s, z_r,
    x2_s, x2_r, z2_s, z2_r, y_s, y_r, f_s, f_r,
):
    dp = lax.axis_index("dp")
    sp = lax.axis_index("space")
    z = dp // 2
    xlo = lax.rem(dp, 2)
    core = lax.rem(sp, 2)
    y = lax.rem(sp // 2, NY)
    x = (sp // (2 * NY)) * 2 + xlo

    def dev(z_, x_, y_, core_):
        return {"dp": z_ * 2 + lax.rem(x_, 2), "space": ((x_ // 2) * NY + y_) * 2 + core_}

    def xp(k):
        return lax.rem(x + k, NX)

    def yp(k):
        return lax.rem(y + k, NY)

    def zp(k):
        return lax.rem(z + k, NZ)

    up = {"dp": dp, "space": lax.rem(sp + 31, 32)}
    down = {"dp": dp, "space": lax.rem(sp + 1, 32)}
    mate = dev(z, x, y, 1 - core)

    barrier = pltpu.get_barrier_semaphore()
    greeted = [dev(zp(k), x, y, core) for k in nearest_last(NZ)]
    greeted += [dev(z, x, yp(k), core) for k in nearest_last(NY)]
    greeted += [dev(z, xp(k), y, core) for k in nearest_last(NX)]
    greeted += [dev(z, xp(k), y, 1 - core) for k in nearest_last(NX)]
    greeted += [up, down]
    for d in greeted:
        pl.semaphore_signal(barrier, inc=1, device_id=d, device_id_type=MESH)

    loads = [
        pltpu.make_async_copy(og_hbm, og_v.at[pl.ds(1, ROWS)], load_sem.at[0]),
        pltpu.make_async_copy(pre_hbm, pre_v, load_sem.at[1]),
        pltpu.make_async_copy(k_hbm, k_v, load_sem.at[2]),
    ]
    loads[0].start()
    loads[1].start()
    og2[pl.ds(3 * C, LANES - 3 * C), :] = jnp.zeros((LANES - 3 * C, (ROWS + 2) * W), BF16)

    def shifts(r, value):
        lanes = pl.ds(r * W, W)
        og2[pl.ds(C, C), lanes] = value
        wide = value.astype(F32)
        col = lax.broadcasted_iota(jnp.int32, (C, W), 1)
        og2[pl.ds(0, C), lanes] = jnp.where(col == W - 1, 0.0, pltpu.roll(wide, W - 1, 1)).astype(BF16)
        og2[pl.ds(2 * C, C), lanes] = jnp.where(col == 0, 0.0, pltpu.roll(wide, 1, 1)).astype(BF16)

    def tap_row(p):
        a = PARTS[p]
        total = lax.dot_general(
            act2[...], og2[:, pl.ds((2 - a) * W, ROWS * W)], (((1,), (1,)), ((), ())), preferred_element_type=F32)
        for t in range(TILES):
            part_sum[p, t] = total[:, t * W : (t + 1) * W]

    def core_copy(p):
        return pltpu.make_async_remote_copy(
            src_ref=part_sum.at[p, pl.ds((1 - core) * NX, NX)], dst_ref=rcv0.at[p], send_sem=c_s.at[p], recv_sem=c_r.at[p],
            device_id=mate, device_id_type=MESH)

    def core_send(p):
        core_copy(p).start()

    def x_slot(ref, p, peer):
        return ref.at[p, peer, :, pl.ds(0, XROWS[p])]

    def z_slot(ref, p, peer):
        return ref.at[p, peer, :, pl.ds(0, ZROWS - XROWS[p])]

    def x2_slot(ref, p, peer):
        return ref.at[p, peer, pl.ds(0, ZROWS - XROWS[p])]

    def z2_slot(ref, p, peer):
        return ref.at[p, peer, pl.ds(0, XROWS[p])]

    def x_copy(p, i, k):
        return pltpu.make_async_remote_copy(
            src_ref=x_slot(snd_x, p, xp(k)), dst_ref=x_slot(rcv_x, p, x), send_sem=x_s.at[p, i], recv_sem=x_r.at[p, x],
            device_id=dev(z, xp(k), y, core), device_id_type=MESH)

    def z_copy(p, i, k):
        return pltpu.make_async_remote_copy(
            src_ref=z_slot(snd_z, p, zp(k)), dst_ref=z_slot(rcv_z, p, z), send_sem=z_s.at[p, i], recv_sem=z_r.at[p, z],
            device_id=dev(zp(k), x, y, core), device_id_type=MESH)

    def x2_copy(p, i, k):
        return pltpu.make_async_remote_copy(
            src_ref=x2_slot(sndx2, p, xp(k)), dst_ref=x2_slot(rcvx2, p, x), send_sem=x2_s.at[p, i], recv_sem=x2_r.at[p, x],
            device_id=dev(z, xp(k), y, core), device_id_type=MESH)

    def z2_copy(p, i, k):
        return pltpu.make_async_remote_copy(
            src_ref=z2_slot(sndz2, p, zp(k)), dst_ref=z2_slot(rcvz2, p, z), send_sem=z2_s.at[p, i], recv_sem=z2_r.at[p, z],
            device_id=dev(zp(k), x, y, core), device_id_type=MESH)

    def arrived(slot, snd, rcv, s_sem, r_sem, p, peer):
        pltpu.make_async_remote_copy(
            src_ref=slot(snd, p, peer), dst_ref=slot(rcv, p, peer), send_sem=s_sem.at[p, 0], recv_sem=r_sem.at[p, peer],
            device_id=mate, device_id_type=MESH).wait_recv()

    def first_send(p):
        core_copy(p).wait_recv()
        for i, k in enumerate(nearest_last(NZ)):
            snd_z[p, zp(k), :, : ZROWS - XROWS[p]] = z_own(p, zp(k)).astype(BF16)
            z_copy(p, i, k).start()
        for i, k in enumerate(nearest_last(NX)):
            snd_x[p, xp(k), :, : XROWS[p]] = x_own(p, xp(k)).astype(BF16)
            x_copy(p, i, k).start()

    def x_own(p, t):
        total = part_sum[p, core * NX + t] + rcv0[p, t]
        return total.reshape(NZ, ZROWS, W)[:, : XROWS[p]]

    def z_own(p, zb):
        rows = pl.ds(pl.multiple_of(zb * ZROWS + XROWS[p], 8), ZROWS - XROWS[p])
        return jnp.stack([
            part_sum[p, core * NX + t, rows, :] + rcv0[p, t, rows, :] for t in range(NX)])

    def x_done(p):
        for k in nearest_last(NX):
            arrived(x_slot, snd_x, rcv_x, x_s, x_r, p, xp(k))
        total = x_own(p, x)
        for k in range(1, NX):
            total = total + rcv_x[p, xp(k), :, : XROWS[p]].astype(F32)
        sndz2[p, :, : XROWS[p]] = total.astype(BF16)
        own2[p, :, : XROWS[p]] = total
        for i, k in enumerate(nearest_last(NZ)):
            z2_copy(p, i, k).start()

    def z_done(p):
        for k in nearest_last(NZ):
            arrived(z_slot, snd_z, rcv_z, z_s, z_r, p, zp(k))
        total = z_own(p, z)
        for k in range(1, NZ):
            total = total + rcv_z[p, zp(k), :, : ZROWS - XROWS[p]].astype(F32)
        sndx2[p, :, : ZROWS - XROWS[p]] = total
        for i, k in enumerate(nearest_last(NX)):
            x2_copy(p, i, k).start()

    def y_copy(p, i, k):
        peer = yp(k)
        return pltpu.make_async_remote_copy(
            src_ref=ybuf.at[p, y], dst_ref=ybuf.at[p, y], send_sem=y_s.at[p, i], recv_sem=y_r.at[p, y],
            device_id=dev(z, x, peer, core), device_id_type=MESH)

    def y_recv(p, k):
        peer = yp(k)
        return pltpu.make_async_remote_copy(
            src_ref=ybuf.at[p, peer], dst_ref=ybuf.at[p, peer], send_sem=y_s.at[p, 0], recv_sem=y_r.at[p, peer],
            device_id=mate, device_id_type=MESH)

    def y_send(p):
        for k in nearest_last(NZ):
            arrived(z2_slot, sndz2, rcvz2, z2_s, z2_r, p, zp(k))
        upper = own2[p, z, : XROWS[p]]
        for k in range(1, NZ):
            upper = upper + rcvz2[p, zp(k), : XROWS[p]].astype(F32)
        for k in nearest_last(NX):
            arrived(x2_slot, sndx2, rcvx2, x2_s, x2_r, p, xp(k))
        lower = sndx2[p, x, : ZROWS - XROWS[p]]
        for k in range(1, NX):
            lower = lower + rcvx2[p, xp(k), : ZROWS - XROWS[p]]
        total = jnp.concatenate([upper, lower], axis=0)
        ybuf[p, y] = (total * scale).astype(BF16)
        for i, k in enumerate(nearest_last(NY)):
            y_copy(p, i, k).start()

    ENDS = [(k, other) for k in (2, 1, 3, 0) for other in (1, 0) if (k, other) != (0, 0)]

    def end_rows(xx):
        return pl.ds(pl.multiple_of(lax.rem(xx, 2) * 16, 8), 24)

    def f_copy(p, i, k, other):
        return pltpu.make_async_remote_copy(
            src_ref=done.at[p, end_rows(xp(k))], dst_ref=fin.at[p, core * NX + x],
            send_sem=f_s.at[p, i], recv_sem=f_r.at[p, core * NX + x],
            device_id=dev(z, xp(k), y, 1 - core if other else core), device_id_type=MESH)

    def f_recv(p, k, other):
        tile = (1 - core if other else core) * NX + xp(k)
        return pltpu.make_async_remote_copy(
            src_ref=done.at[p, end_rows(x)], dst_ref=fin.at[p, tile],
            send_sem=f_s.at[p, 0], recv_sem=f_r.at[p, tile], device_id=mate, device_id_type=MESH)

    def f_send(p):
        for k in nearest_last(NY):
            y_recv(p, k).wait_recv()
        total = ybuf[p, 0].astype(F32)
        for yy in range(1, NY):
            total = total + ybuf[p, yy].astype(F32)
        done[p] = total
        for i, (k, other) in enumerate(ENDS):
            f_copy(p, i, k, other).start()
        fin[p, core * NX + x] = done[p, end_rows(x), :]

    def finish(p):
        for k, other in ENDS:
            f_recv(p, k, other).wait_recv()
        wide = jnp.concatenate([fin[p, t] for t in range(TILES)], axis=1)
        wide = jnp.where(xlo == 0, wide[:BLK], wide[4 : 4 + BLK])
        for b in range(3):
            tap = wide[:, b * C : b * C + 3 * W]
            for t in range(3):
                kg_v[t, pl.ds(PARTS[p] * 3 + b, BLK, stride=9), :] = tap[:, t * W : (t + 1) * W]

    def in_grad(pair):
        lanes = pair * 2 * W
        total = jnp.zeros((C, 2 * W), F32)
        for a in range(3):
            for b in range(3):
                total = total + jnp.dot(
                    k_v[a, b], og2[pl.ds(b * C, C), pl.ds((2 - a) * W + lanes, 2 * W)], preferred_element_type=F32)
        for i in range(2):
            v = pre_v[pair * 2 + i].astype(F32)
            s = 1.0 / (1.0 + jnp.exp(-v))
            in_v[pair * 2 + i] = (total[:, i * W : (i + 1) * W] * (s * (1.0 + v * (1.0 - s)))).astype(BF16)

    halos = [
        pltpu.make_async_remote_copy(
            src_ref=og_hbm.at[ROWS - 1], dst_ref=og_v.at[0], send_sem=halo_s.at[0], recv_sem=halo_r.at[0],
            device_id=down, device_id_type=MESH),
        pltpu.make_async_remote_copy(
            src_ref=og_hbm.at[0], dst_ref=og_v.at[ROWS + 1], send_sem=halo_s.at[1], recv_sem=halo_r.at[1],
            device_id=up, device_id_type=MESH),
    ]

    loads[0].wait()
    for r in range(1, ROWS + 1):
        shifts(r, og_v[r])
    loads[1].wait()
    loads[2].start()
    for r in range(ROWS):
        v = pre_v[r].astype(F32)
        act2[:, pl.ds(r * W, W)] = (v * (1.0 / (1.0 + jnp.exp(-v)))).astype(BF16)
    tap_row(0)
    pl.semaphore_wait(barrier, len(greeted))
    for c in halos:
        c.start()
    core_send(0)
    first_send(0)
    for i, (c, edge) in enumerate(zip(halos, (sp == 0, sp == 31))):
        c.wait_recv()
        r = i * (ROWS + 1)
        shifts(r, jnp.where(edge, jnp.zeros((C, W), BF16), og_v[r]))
    tap_row(1)
    core_send(1)
    tap_row(2)
    core_send(2)
    first_send(1)
    first_send(2)
    loads[2].wait()
    for q in range(4):
        in_grad(q)
    in_store = pltpu.make_async_copy(in_v, in_hbm, store_sem.at[0])
    in_store.start()
    x_done(0)
    z_done(0)
    x_done(1)
    x_done(2)
    z_done(1)
    z_done(2)
    for p in range(3):
        y_send(p)
    for p in range(3):
        f_send(p)
    for p in range(3):
        finish(p)
    kg_stores = [
        pltpu.make_async_copy(kg_v.at[t], kg_hbm.at[:, pl.ds(t * W, W)], store_sem.at[1 + t]) for t in range(3)
    ]
    for c in kg_stores:
        c.start()

    for c in halos:
        c.wait_send()
    for p in range(3):
        core_copy(p).wait_send()
        for i, k in enumerate(nearest_last(NX)):
            x_copy(p, i, k).wait_send()
            x2_copy(p, i, k).wait_send()
        for i, k in enumerate(nearest_last(NZ)):
            z_copy(p, i, k).wait_send()
            z2_copy(p, i, k).wait_send()
        for i, k in enumerate(nearest_last(NY)):
            y_copy(p, i, k).wait_send()
        for i, (k, other) in enumerate(ENDS):
            f_copy(p, i, k, other).wait_send()
    in_store.wait()
    for c in kg_stores:
        c.wait()


def shards(scale, pre_act, out_grad, weights):
    to_rows = lambda t: jnp.swapaxes(t[0], 1, 2)
    vm, sem = pltpu.VMEM, pltpu.SemaphoreType.DMA
    grad, kernel_grad = pl.pallas_call(
        functools.partial(kernel, scale),
        out_shape=(
            jax.ShapeDtypeStruct((ROWS, C, W), BF16),
            jax.ShapeDtypeStruct((9 * BLK, 3 * W), F32),
        ),
        in_specs=[pl.BlockSpec(memory_space=pl.ANY)] * 3,
        out_specs=(pl.BlockSpec(memory_space=pl.ANY),) * 2,
        scratch_shapes=[
            vm((ROWS, C, W), BF16),
            vm((ROWS + 2, C, W), BF16),
            vm((3, 3, C, C), BF16),
            vm((ROWS, C, W), BF16),
            vm((3, 9 * BLK, W), F32),
            vm((C, ROWS * W), BF16),
            vm((LANES, (ROWS + 2) * W), BF16),
            vm((3, TILES, C, W), F32),
            vm((3, NX, C, W), F32),
            vm((3, NX, NZ, max(XROWS), W), BF16),
            vm((3, NX, NZ, max(XROWS), W), BF16),
            vm((3, NZ, NX, ZROWS - min(XROWS), W), BF16),
            vm((3, NZ, NX, ZROWS - min(XROWS), W), BF16),
            vm((3, NX, ZROWS - min(XROWS), W), F32),
            vm((3, NX, ZROWS - min(XROWS), W), F32),
            vm((3, NZ, max(XROWS), W), BF16),
            vm((3, NZ, max(XROWS), W), BF16),
            vm((3, NZ, max(XROWS), W), F32),
            vm((3, NY, ZROWS, W), BF16),
            vm((3, ZROWS, W), F32),
            vm((3, TILES, 24, W), F32),
            sem((3,)), sem((4,)), sem((2,)), sem((2,)), sem((3,)), sem((3,)),
            sem((3, 3)), sem((3, NX)), sem((3, 7)), sem((3, NZ)),
            sem((3, 3)), sem((3, NX)), sem((3, 7)), sem((3, NZ)),
            sem((3, 7)), sem((3, NY)), sem((3, 7)), sem((3, TILES)),
        ],
        compiler_params=pltpu.CompilerParams(collective_id=0, has_side_effects=True),
    )(to_rows(pre_act), to_rows(out_grad), weights)
    return jnp.swapaxes(grad, 1, 2)[None], kernel_grad[:, :C]


def solution(mesh):
    placed = P("dp", "space", None, None)

    def whole(pre_act, out_grad, weights):
        pixels = pre_act.shape[0] * pre_act.shape[1] * pre_act.shape[2]
        return jax.shard_map(
            functools.partial(shards, float(pixels) ** -0.5),
            mesh=mesh,
            in_specs=(placed, placed, P()),
            out_specs=(placed, P("dp", None)),
            check_vma=False,
        )(pre_act, out_grad, weights)

    return whole
```

```python
import functools

import jax
import jax.numpy as jnp
from jax import lax
from jax.experimental import pallas as pl
from jax.experimental.pallas import tpu as pltpu
from jax.sharding import PartitionSpec as P

MESH = pl.DeviceIdType.MESH
F32 = jnp.float32
BF16 = jnp.bfloat16

NX, NY, NZ = 4, 8, 8
ROWS, C, W = 8, 320, 128
BLK = 20
ZROWS = 2 * BLK
LANES, TILES = 1024, 8
BF16, SECOND_T, BF16 = BF16, F32, BF16
PARTS = (1, 0, 2)
ZROWS = 2 * BLK
XROWS = (16, 32, 24)
LANES, TILES = 1024, 8


def nearest_last(n):
    steps = []
    for k in range(n // 2, 0, -1):
        steps.append(k)
        if n - k != k:
            steps.append(n - k)
    return steps


def kernel(
    scale, pre_hbm, og_hbm, k_hbm, in_hbm, kg_hbm,
    pre_v, og_v, k_v, in_v, kg_v, act2, og2, part_sum,
    rcv0, snd_x, rcv_x, snd_z, rcv_z,
    sndx2, rcvx2, sndz2, rcvz2, own2, ybuf, done, fin,
    load_sem, store_sem, halo_s, halo_r, c_s, c_r, x_s, x_r, z_s, z_r,
    x2_s, x2_r, z2_s, z2_r, y_s, y_r, f_s, f_r,
):
    dp = lax.axis_index("dp")
    sp = lax.axis_index("space")
    z = dp // 2
    xlo = lax.rem(dp, 2)
    core = lax.rem(sp, 2)
    y = lax.rem(sp // 2, NY)
    x = (sp // (2 * NY)) * 2 + xlo

    def dev(z_, x_, y_, core_):
        return {"dp": z_ * 2 + lax.rem(x_, 2), "space": ((x_ // 2) * NY + y_) * 2 + core_}

    def xp(k):
        return lax.rem(x + k, NX)

    def yp(k):
        return lax.rem(y + k, NY)

    def zp(k):
        return lax.rem(z + k, NZ)

    up = {"dp": dp, "space": lax.rem(sp + 31, 32)}
    down = {"dp": dp, "space": lax.rem(sp + 1, 32)}
    mate = dev(z, x, y, 1 - core)

    barrier = pltpu.get_barrier_semaphore()
    greeted = [dev(zp(k), x, y, core) for k in nearest_last(NZ)]
    greeted += [dev(z, x, yp(k), core) for k in nearest_last(NY)]
    greeted += [dev(z, xp(k), y, core) for k in nearest_last(NX)]
    greeted += [dev(z, xp(k), y, 1 - core) for k in nearest_last(NX)]
    greeted += [up, down]
    for d in greeted:
        pl.semaphore_signal(barrier, inc=1, device_id=d, device_id_type=MESH)

    loads = [
        pltpu.make_async_copy(og_hbm, og_v.at[pl.ds(1, ROWS)], load_sem.at[0]),
        pltpu.make_async_copy(pre_hbm, pre_v, load_sem.at[1]),
        pltpu.make_async_copy(k_hbm, k_v, load_sem.at[2]),
    ]
    loads[0].start()
    loads[1].start()
    og2[pl.ds(3 * C, LANES - 3 * C), :] = jnp.zeros((LANES - 3 * C, (ROWS + 2) * W), BF16)

    def shifts(r, value):
        lanes = pl.ds(r * W, W)
        og2[pl.ds(C, C), lanes] = value
        wide = value.astype(F32)
        col = lax.broadcasted_iota(jnp.int32, (C, W), 1)
        og2[pl.ds(0, C), lanes] = jnp.where(col == W - 1, 0.0, pltpu.roll(wide, W - 1, 1)).astype(BF16)
        og2[pl.ds(2 * C, C), lanes] = jnp.where(col == 0, 0.0, pltpu.roll(wide, 1, 1)).astype(BF16)

    def product(act_lanes, og_lanes):
        return lax.dot_general(
            act2[:, act_lanes], og2[:, og_lanes], (((1,), (1,)), ((), ())), preferred_element_type=F32)

    def tap_row(p):
        a = PARTS[p]
        first = 1 if a == 2 else 0
        count = ROWS if a == 1 else ROWS - 1
        total = product(pl.ds(first * W, count * W), pl.ds((first + 2 - a) * W, count * W))
        for t in range(TILES):
            part_sum[p, t] = total[:, t * W : (t + 1) * W]

    def edge_row(p):
        a = PARTS[p]
        row = 0 if a == 2 else ROWS - 1
        total = product(pl.ds(row * W, W), pl.ds((row + 2 - a) * W, W))
        for t in range(TILES):
            part_sum[p, t] += total[:, t * W : (t + 1) * W]

    def core_copy(p):
        return pltpu.make_async_remote_copy(
            src_ref=part_sum.at[p, pl.ds((1 - core) * NX, NX)], dst_ref=rcv0.at[p], send_sem=c_s.at[p], recv_sem=c_r.at[p],
            device_id=mate, device_id_type=MESH)

    def core_send(p):
        core_copy(p).start()

    def x_slot(ref, p, peer):
        return ref.at[p, peer, :, pl.ds(0, XROWS[p])]

    def z_slot(ref, p, peer):
        return ref.at[p, peer, :, pl.ds(0, ZROWS - XROWS[p])]

    def x2_slot(ref, p, peer):
        return ref.at[p, peer, pl.ds(0, ZROWS - XROWS[p])]

    def z2_slot(ref, p, peer):
        return ref.at[p, peer, pl.ds(0, XROWS[p])]

    def x_copy(p, i, k):
        return pltpu.make_async_remote_copy(
            src_ref=x_slot(snd_x, p, xp(k)), dst_ref=x_slot(rcv_x, p, x), send_sem=x_s.at[p, i], recv_sem=x_r.at[p, x],
            device_id=dev(z, xp(k), y, core), device_id_type=MESH)

    def z_copy(p, i, k):
        return pltpu.make_async_remote_copy(
            src_ref=z_slot(snd_z, p, zp(k)), dst_ref=z_slot(rcv_z, p, z), send_sem=z_s.at[p, i], recv_sem=z_r.at[p, z],
            device_id=dev(zp(k), x, y, core), device_id_type=MESH)

    def x2_copy(p, i, k):
        return pltpu.make_async_remote_copy(
            src_ref=x2_slot(sndx2, p, xp(k)), dst_ref=x2_slot(rcvx2, p, x), send_sem=x2_s.at[p, i], recv_sem=x2_r.at[p, x],
            device_id=dev(z, xp(k), y, core), device_id_type=MESH)

    def z2_copy(p, i, k):
        return pltpu.make_async_remote_copy(
            src_ref=z2_slot(sndz2, p, zp(k)), dst_ref=z2_slot(rcvz2, p, z), send_sem=z2_s.at[p, i], recv_sem=z2_r.at[p, z],
            device_id=dev(zp(k), x, y, core), device_id_type=MESH)

    def arrived(slot, snd, rcv, s_sem, r_sem, p, peer):
        pltpu.make_async_remote_copy(
            src_ref=slot(snd, p, peer), dst_ref=slot(rcv, p, peer), send_sem=s_sem.at[p, 0], recv_sem=r_sem.at[p, peer],
            device_id=mate, device_id_type=MESH).wait_recv()

    def first_send(p):
        core_copy(p).wait_recv()
        for i, k in enumerate(nearest_last(NZ)):
            snd_z[p, zp(k), :, : ZROWS - XROWS[p]] = z_own(p, zp(k)).astype(BF16)
            z_copy(p, i, k).start()
        for i, k in enumerate(nearest_last(NX)):
            snd_x[p, xp(k), :, : XROWS[p]] = x_own(p, xp(k)).astype(BF16)
            x_copy(p, i, k).start()

    def x_own(p, t):
        total = part_sum[p, core * NX + t] + rcv0[p, t]
        return total.reshape(NZ, ZROWS, W)[:, : XROWS[p]]

    def z_own(p, zb):
        rows = pl.ds(pl.multiple_of(zb * ZROWS + XROWS[p], 8), ZROWS - XROWS[p])
        return jnp.stack([
            part_sum[p, core * NX + t, rows, :] + rcv0[p, t, rows, :] for t in range(NX)])

    def x_done(p):
        for k in nearest_last(NX):
            arrived(x_slot, snd_x, rcv_x, x_s, x_r, p, xp(k))
        total = x_own(p, x)
        for k in range(1, NX):
            total = total + rcv_x[p, xp(k), :, : XROWS[p]].astype(F32)
        sndz2[p, :, : XROWS[p]] = total.astype(BF16)
        own2[p, :, : XROWS[p]] = total
        for i, k in enumerate(nearest_last(NZ)):
            z2_copy(p, i, k).start()

    def z_done(p):
        for k in nearest_last(NZ):
            arrived(z_slot, snd_z, rcv_z, z_s, z_r, p, zp(k))
        total = z_own(p, z)
        for k in range(1, NZ):
            total = total + rcv_z[p, zp(k), :, : ZROWS - XROWS[p]].astype(F32)
        sndx2[p, :, : ZROWS - XROWS[p]] = total
        for i, k in enumerate(nearest_last(NX)):
            x2_copy(p, i, k).start()

    def y_copy(p, i, k):
        peer = yp(k)
        return pltpu.make_async_remote_copy(
            src_ref=ybuf.at[p, y], dst_ref=ybuf.at[p, y], send_sem=y_s.at[p, i], recv_sem=y_r.at[p, y],
            device_id=dev(z, x, peer, core), device_id_type=MESH)

    def y_recv(p, k):
        peer = yp(k)
        return pltpu.make_async_remote_copy(
            src_ref=ybuf.at[p, peer], dst_ref=ybuf.at[p, peer], send_sem=y_s.at[p, 0], recv_sem=y_r.at[p, peer],
            device_id=mate, device_id_type=MESH)

    def y_send(p):
        for k in nearest_last(NZ):
            arrived(z2_slot, sndz2, rcvz2, z2_s, z2_r, p, zp(k))
        upper = own2[p, z, : XROWS[p]]
        for k in range(1, NZ):
            upper = upper + rcvz2[p, zp(k), : XROWS[p]].astype(F32)
        for k in nearest_last(NX):
            arrived(x2_slot, sndx2, rcvx2, x2_s, x2_r, p, xp(k))
        lower = sndx2[p, x, : ZROWS - XROWS[p]]
        for k in range(1, NX):
            lower = lower + rcvx2[p, xp(k), : ZROWS - XROWS[p]]
        total = jnp.concatenate([upper, lower], axis=0)
        ybuf[p, y] = (total * scale).astype(BF16)
        for i, k in enumerate(nearest_last(NY)):
            y_copy(p, i, k).start()

    ENDS = [(k, other) for k in (2, 1, 3, 0) for other in (1, 0) if (k, other) != (0, 0)]

    def end_rows(xx):
        return pl.ds(pl.multiple_of(lax.rem(xx, 2) * 16, 8), 24)

    def f_copy(p, i, k, other):
        return pltpu.make_async_remote_copy(
            src_ref=done.at[p, end_rows(xp(k))], dst_ref=fin.at[p, core * NX + x],
            send_sem=f_s.at[p, i], recv_sem=f_r.at[p, core * NX + x],
            device_id=dev(z, xp(k), y, 1 - core if other else core), device_id_type=MESH)

    def f_recv(p, k, other):
        tile = (1 - core if other else core) * NX + xp(k)
        return pltpu.make_async_remote_copy(
            src_ref=done.at[p, end_rows(x)], dst_ref=fin.at[p, tile],
            send_sem=f_s.at[p, 0], recv_sem=f_r.at[p, tile], device_id=mate, device_id_type=MESH)

    def f_send(p):
        for k in nearest_last(NY):
            y_recv(p, k).wait_recv()
        total = ybuf[p, 0].astype(F32)
        for yy in range(1, NY):
            total = total + ybuf[p, yy].astype(F32)
        done[p] = total
        for i, (k, other) in enumerate(ENDS):
            f_copy(p, i, k, other).start()
        fin[p, core * NX + x] = done[p, end_rows(x), :]

    def finish(p):
        for k, other in ENDS:
            f_recv(p, k, other).wait_recv()
        wide = jnp.concatenate([fin[p, t] for t in range(TILES)], axis=1)
        wide = jnp.where(xlo == 0, wide[:BLK], wide[4 : 4 + BLK])
        for b in range(3):
            tap = wide[:, b * C : b * C + 3 * W]
            for t in range(3):
                kg_v[t, pl.ds(PARTS[p] * 3 + b, BLK, stride=9), :] = tap[:, t * W : (t + 1) * W]

    def in_grad(pair):
        lanes = pair * 2 * W
        total = jnp.zeros((C, 2 * W), F32)
        for a in range(3):
            for b in range(3):
                total = total + jnp.dot(
                    k_v[a, b], og2[pl.ds(b * C, C), pl.ds((2 - a) * W + lanes, 2 * W)], preferred_element_type=F32)
        for i in range(2):
            v = pre_v[pair * 2 + i].astype(F32)
            s = 1.0 / (1.0 + jnp.exp(-v))
            in_v[pair * 2 + i] = (total[:, i * W : (i + 1) * W] * (s * (1.0 + v * (1.0 - s)))).astype(BF16)

    halos = [
        pltpu.make_async_remote_copy(
            src_ref=og_hbm.at[ROWS - 1], dst_ref=og_v.at[0], send_sem=halo_s.at[0], recv_sem=halo_r.at[0],
            device_id=down, device_id_type=MESH),
        pltpu.make_async_remote_copy(
            src_ref=og_hbm.at[0], dst_ref=og_v.at[ROWS + 1], send_sem=halo_s.at[1], recv_sem=halo_r.at[1],
            device_id=up, device_id_type=MESH),
    ]

    loads[0].wait()
    for r in range(1, ROWS + 1):
        shifts(r, og_v[r])
    loads[1].wait()
    loads[2].start()
    for r in range(ROWS):
        v = pre_v[r].astype(F32)
        act2[:, pl.ds(r * W, W)] = (v * (1.0 / (1.0 + jnp.exp(-v)))).astype(BF16)
    tap_row(0)
    pl.semaphore_wait(barrier, len(greeted))
    for c in halos:
        c.start()
    core_send(0)
    tap_row(1)
    first_send(0)
    tap_row(2)
    for i, (c, edge) in enumerate(zip(halos, (sp == 0, sp == 31))):
        c.wait_recv()
        r = i * (ROWS + 1)
        shifts(r, jnp.where(edge, jnp.zeros((C, W), BF16), og_v[r]))
    edge_row(1)
    core_send(1)
    edge_row(2)
    core_send(2)
    first_send(1)
    first_send(2)
    loads[2].wait()
    for q in range(4):
        in_grad(q)
    in_store = pltpu.make_async_copy(in_v, in_hbm, store_sem.at[0])
    in_store.start()
    x_done(0)
    z_done(0)
    x_done(1)
    x_done(2)
    z_done(1)
    z_done(2)
    for p in range(3):
        y_send(p)
    for p in range(3):
        f_send(p)
    for p in range(3):
        finish(p)
    kg_stores = [
        pltpu.make_async_copy(kg_v.at[t], kg_hbm.at[:, pl.ds(t * W, W)], store_sem.at[1 + t]) for t in range(3)
    ]
    for c in kg_stores:
        c.start()

    for c in halos:
        c.wait_send()
    for p in range(3):
        core_copy(p).wait_send()
        for i, k in enumerate(nearest_last(NX)):
            x_copy(p, i, k).wait_send()
            x2_copy(p, i, k).wait_send()
        for i, k in enumerate(nearest_last(NZ)):
            z_copy(p, i, k).wait_send()
            z2_copy(p, i, k).wait_send()
        for i, k in enumerate(nearest_last(NY)):
            y_copy(p, i, k).wait_send()
        for i, (k, other) in enumerate(ENDS):
            f_copy(p, i, k, other).wait_send()
    in_store.wait()
    for c in kg_stores:
        c.wait()


def shards(scale, pre_act, out_grad, weights):
    to_rows = lambda t: jnp.swapaxes(t[0], 1, 2)
    vm, sem = pltpu.VMEM, pltpu.SemaphoreType.DMA
    grad, kernel_grad = pl.pallas_call(
        functools.partial(kernel, scale),
        out_shape=(
            jax.ShapeDtypeStruct((ROWS, C, W), BF16),
            jax.ShapeDtypeStruct((9 * BLK, 3 * W), F32),
        ),
        in_specs=[pl.BlockSpec(memory_space=pl.ANY)] * 3,
        out_specs=(pl.BlockSpec(memory_space=pl.ANY),) * 2,
        scratch_shapes=[
            vm((ROWS, C, W), BF16),
            vm((ROWS + 2, C, W), BF16),
            vm((3, 3, C, C), BF16),
            vm((ROWS, C, W), BF16),
            vm((3, 9 * BLK, W), F32),
            vm((C, ROWS * W), BF16),
            vm((LANES, (ROWS + 2) * W), BF16),
            vm((3, TILES, C, W), F32),
            vm((3, NX, C, W), F32),
            vm((3, NX, NZ, max(XROWS), W), BF16),
            vm((3, NX, NZ, max(XROWS), W), BF16),
            vm((3, NZ, NX, ZROWS - min(XROWS), W), BF16),
            vm((3, NZ, NX, ZROWS - min(XROWS), W), BF16),
            vm((3, NX, ZROWS - min(XROWS), W), F32),
            vm((3, NX, ZROWS - min(XROWS), W), F32),
            vm((3, NZ, max(XROWS), W), BF16),
            vm((3, NZ, max(XROWS), W), BF16),
            vm((3, NZ, max(XROWS), W), F32),
            vm((3, NY, ZROWS, W), BF16),
            vm((3, ZROWS, W), F32),
            vm((3, TILES, 24, W), F32),
            sem((3,)), sem((4,)), sem((2,)), sem((2,)), sem((3,)), sem((3,)),
            sem((3, 3)), sem((3, NX)), sem((3, 7)), sem((3, NZ)),
            sem((3, 3)), sem((3, NX)), sem((3, 7)), sem((3, NZ)),
            sem((3, 7)), sem((3, NY)), sem((3, 7)), sem((3, TILES)),
        ],
        compiler_params=pltpu.CompilerParams(collective_id=0, has_side_effects=True),
    )(to_rows(pre_act), to_rows(out_grad), weights)
    return jnp.swapaxes(grad, 1, 2)[None], kernel_grad[:, :C]


def solution(mesh):
    placed = P("dp", "space", None, None)

    def whole(pre_act, out_grad, weights):
        pixels = pre_act.shape[0] * pre_act.shape[1] * pre_act.shape[2]
        return jax.shard_map(
            functools.partial(shards, float(pixels) ** -0.5),
            mesh=mesh,
            in_specs=(placed, placed, P()),
            out_specs=(placed, P("dp", None)),
            check_vma=False,
        )(pre_act, out_grad, weights)

    return whole
```
